32 devices in a mesh: tm: 8 (over z, x), space: 4 (over y, core).
Axes of the slice: x: 2, y: 2, z: 4, core: 2. Of those that a mesh axis runs over, the one named last changes fastest.
Arguments:
- queries: bfloat16 [8, 512, 2048], P('tm', 'space'), may hold values from -180 to 180
- key_vectors: bfloat16 [8, 512, 2048], P('tm', 'space'), may hold values from -6 to 6
- value_vectors: bfloat16 [8, 512, 2048], P('tm', 'space'), may hold values from -96 to 96
- block_lists: int32 [4, 3], replicated, may hold values from 0 to 3, as said below
- step_sizes: float32 [8, 512, 16], P(None, ('space', 'tm')), may hold values from 0.004 to 0.6, as said below
- decay_rates: float32 [16], replicated, may hold values from 0.7 to 1.4
- skip_gains: float32 [16], replicated, may hold values from 0.5 to 1.5
- pre_gain: float32 [2048], replicated, may hold values from 0.25 to 1.75
- state_in_weight: bfloat16 [2048, 64], replicated, may hold values from -0.125 to 0.125
- state_out_weight: bfloat16 [2048, 64], replicated, may hold values from -0.125 to 0.125
- post_gain: float32 [2048], replicated, may hold values from 0.25 to 1.75
Outputs:
- mixed_out: bfloat16 [8, 512, 2048], P('tm', 'space')
The draws below stay inside these ranges and needn't reach their ends.
Inputs may be any that keep to these rules, and one draw needn't show every extreme that they name: `block_lists`: row i lists 3 different key blocks; its first entry is i itself. `step_sizes`: positive step sizes.
All inputs are finite; a program needn't handle non-finite values.
Results may differ from the reference program's by a relative error of at most 0.01.
Values may be sent and summed in bfloat16 or wider, within the bound.
A program may use at most 64 MiB of HBM per device.

```python
import math
from functools import partial
import jax
import jax.numpy as jnp
from jax import lax

SHARED_HEADS = 16
HEAD_DIM = 128
STATE = 64
BLOCK = 128
LATENT_FRAMES = 8
FTOK = 512
NBLK = 4
KSEL = 3
HD = 2048


def paired_states(base_key):
    own_key = jax.random.fold_in(base_key, 17)
    key_q, key_k = jax.random.split(own_key, 2)
    full_shape = (LATENT_FRAMES, FTOK, SHARED_HEADS * HEAD_DIM)
    query_draw = jnp.clip(jax.random.normal(key_q, full_shape, jnp.float32), -6.0, 6.0)
    key_draw = jnp.clip(jax.random.normal(key_k, full_shape, jnp.float32), -6.0, 6.0)
    return (query_draw, key_draw)


def draw_queries(key, part):
    return paired_states(key)[0].astype(jnp.bfloat16)


def draw_key_vectors(key, part):
    return paired_states(key)[1].astype(jnp.bfloat16)


def draw_value_vectors(key, part):
    own_key = jax.random.fold_in(key, 23)
    key_a, key_b, key_c = jax.random.split(own_key, 3)
    full_shape = (LATENT_FRAMES, FTOK, SHARED_HEADS * HEAD_DIM)
    frame_scale = jnp.exp(jax.random.uniform(key_a, (LATENT_FRAMES, 1, 1), jnp.float32, math.log(0.4), math.log(4.0)))
    column_scale = jnp.exp(jax.random.uniform(key_b, (1, 1, SHARED_HEADS * HEAD_DIM), jnp.float32, math.log(0.4), math.log(4.0)))
    core = jnp.clip(jax.random.normal(key_c, full_shape, jnp.float32), -6.0, 6.0)
    return (core * frame_scale * column_scale).astype(jnp.bfloat16)


def draw_block_lists(key, part):
    own_key = jax.random.fold_in(key, 29)
    rank_keys = jax.random.randint(own_key, (NBLK, NBLK), 0, 2 ** 20) * NBLK + jnp.arange(NBLK)[None, :]
    rank_keys = jnp.where(jnp.eye(NBLK, dtype=bool), -1, rank_keys)
    ordering = jnp.argsort(rank_keys, axis=1, stable=True)
    return ordering[:, :KSEL].astype(jnp.int32)


def draw_step_sizes(key, part):
    own_key = jax.random.fold_in(key, 31)
    key_a, key_b, key_c, key_d, random_key_fifth, random_key_sixth = jax.random.split(own_key, 6)
    full_shape = (LATENT_FRAMES, FTOK, SHARED_HEADS)
    fast_count = SHARED_HEADS // 2
    fast_heads = jax.random.permutation(key_a, SHARED_HEADS) < fast_count
    slow_rate = jnp.exp(jax.random.uniform(key_b, (SHARED_HEADS,), jnp.float32, math.log(0.008), math.log(0.02)))
    fast_rate = jnp.exp(jax.random.uniform(key_c, (SHARED_HEADS,), jnp.float32, math.log(0.12), math.log(0.3)))
    baseline_rate = jnp.where(fast_heads, fast_rate, slow_rate)
    jaggedness = jnp.exp(jax.random.uniform(key_d, full_shape, jnp.float32, math.log(0.5), math.log(2.0)))
    spike_frames = jax.random.randint(random_key_fifth, (2, SHARED_HEADS), 0, LATENT_FRAMES)
    spike_mask = jnp.any(jnp.arange(LATENT_FRAMES)[None, :, None] == spike_frames[:, None, :], axis=0)
    spike_length = jax.random.uniform(random_key_sixth, (LATENT_FRAMES, SHARED_HEADS), jnp.float32, 0.3, 0.5)
    return jnp.where(spike_mask[:, None, :], spike_length[:, None, :], baseline_rate * jaggedness)


def normal_values(stream_key, dims, scale, reach, held_as=jnp.bfloat16):
    entries = jax.random.normal(stream_key, dims, jnp.float32) * scale
    return jnp.minimum(jnp.maximum(entries, -reach), reach).astype(held_as)


def setup_inputs(seed: int = 0) -> dict:
    key_list = jax.random.split(jax.random.key(seed), 12)
    return {
        "queries": draw_queries(jax.random.fold_in(key_list[11], 71), 0),
        "key_vectors": draw_key_vectors(jax.random.fold_in(key_list[11], 71), 0),
        "value_vectors": draw_value_vectors(jax.random.fold_in(key_list[11], 71), 0),
        "block_lists": draw_block_lists(jax.random.fold_in(key_list[11], 71), 0),
        "step_sizes": draw_step_sizes(jax.random.fold_in(key_list[11], 71), 0),
        "decay_rates": jnp.clip(jnp.exp(jax.random.uniform(key_list[5], (SHARED_HEADS,), jnp.float32, math.log(0.7), math.log(1.4))), 0.7, 1.4),
        "skip_gains": jnp.clip(jax.random.uniform(key_list[6], (SHARED_HEADS,), jnp.float32, 0.5, 1.5), 0.5, 1.5),
        "pre_gain": jnp.clip(1.0 + 0.15 * jax.random.normal(key_list[7], (HD,), jnp.float32), 0.25, 1.75),
        "state_in_weight": normal_values(key_list[8], (HD, STATE), HD ** -0.5, 0.125),
        "state_out_weight": normal_values(key_list[9], (HD, STATE), HD ** -0.5, 0.125),
        "post_gain": jnp.clip(1.0 + 0.15 * jax.random.normal(key_list[10], (HD,), jnp.float32), 0.25, 1.75),
    }


def rms_scale(values, gain_row):
    return values * lax.rsqrt(lax.optimization_barrier(jnp.mean(values * values, axis=-1, keepdims=True)) + 1e-05) * gain_row

def attend_frame(frame_arrays, block_lists):
    query_frame, key_frame, value_frame = frame_arrays
    block_count = FTOK // BLOCK
    group_size = math.gcd(block_count, max(1, 512 // BLOCK))
    list_width = block_lists.shape[1]
    score_scale = 1.0 / math.sqrt(HEAD_DIM)
    query_blocks = query_frame.reshape(block_count, BLOCK, SHARED_HEADS, HEAD_DIM)
    key_blocks = key_frame.reshape(block_count, BLOCK, SHARED_HEADS, HEAD_DIM)
    value_blocks = value_frame.reshape(block_count, BLOCK, SHARED_HEADS, HEAD_DIM)

    def attend_group(group_index):
        first_block = (group_index * group_size).astype(jnp.int32)
        chosen = lax.dynamic_slice_in_dim(block_lists, first_block, group_size, 0)
        query_group = lax.dynamic_slice_in_dim(query_blocks, first_block, group_size, 0).astype(jnp.float32)
        key_group = jnp.take(key_blocks, chosen, axis=0).reshape(group_size, list_width * BLOCK, SHARED_HEADS, HEAD_DIM).astype(jnp.float32)
        value_group = jnp.take(value_blocks, chosen, axis=0).reshape(group_size, list_width * BLOCK, SHARED_HEADS, HEAD_DIM).astype(jnp.float32)
        scores = jnp.einsum('gqhd,gkhd->ghqk', query_group, key_group) * score_scale
        row_max = lax.optimization_barrier(jnp.max(scores, axis=-1, keepdims=True))
        exp_scores = jnp.exp(scores - row_max)
        totals = lax.optimization_barrier(jnp.sum(exp_scores, axis=-1))
        weights_bf = lax.optimization_barrier(exp_scores.astype(jnp.bfloat16)).astype(jnp.float32)
        summed = jnp.einsum('ghqk,gkhd->gqhd', weights_bf, value_group)
        return (summed / jnp.transpose(totals, (0, 2, 1))[..., None]).astype(jnp.bfloat16)
    attended = lax.map(attend_group, jnp.arange(block_count // group_size, dtype=jnp.int32))
    return attended.reshape(FTOK, SHARED_HEADS * HEAD_DIM)

def temporal_mix(normed, step_block, decay_rates, skip_gains, state_in_weight, state_out_weight, post_gain):
    frame_count, token_count, channel_count = normed.shape
    head_count = step_block.shape[2]
    head_width = channel_count // head_count
    flat_rows = normed.reshape(frame_count * token_count, channel_count)
    b_in = jnp.dot(flat_rows, state_in_weight, preferred_element_type=jnp.float32).reshape(frame_count, token_count, -1)
    c_out = jnp.dot(flat_rows, state_out_weight, preferred_element_type=jnp.float32).reshape(frame_count, token_count, -1)
    gram_matrix = jnp.einsum('tkn,skn->kts', c_out, b_in, precision=lax.Precision.HIGHEST)
    log_decay = -step_block * decay_rates
    frame_index = jnp.arange(frame_count, dtype=jnp.int32)
    between = ((frame_index[None, :, None] < frame_index[None, None, :]) & (frame_index[None, None, :] <= frame_index[:, None, None])).astype(jnp.float32)
    seg_sum = jnp.einsum('tsr,rkh->ktsh', between, log_decay, precision=lax.Precision.HIGHEST)
    causal = frame_index[None, :] <= frame_index[:, None]
    decay_matrix = jnp.where(causal[None, :, :, None], jnp.exp(seg_sum), jnp.zeros_like(seg_sum))
    weight_matrix = gram_matrix[..., None] * decay_matrix * jnp.transpose(step_block, (1, 0, 2))[:, None, :, :]
    x_values = normed.astype(jnp.float32).reshape(frame_count, token_count, head_count, head_width)
    y_mixed = jnp.einsum('ktsh,skhp->tkhp', weight_matrix, x_values, precision=lax.Precision.HIGHEST) + skip_gains[:, None] * x_values
    y_flat = y_mixed.reshape(frame_count, token_count, channel_count)
    return rms_scale(y_flat, post_gain).astype(jnp.bfloat16)

def reference(queries, key_vectors, value_vectors, block_lists, step_sizes, decay_rates, skip_gains, pre_gain, state_in_weight, state_out_weight, post_gain):
    attended = lax.map(partial(attend_frame, block_lists=block_lists), (queries, key_vectors, value_vectors))
    normed = rms_scale(attended.astype(jnp.float32), pre_gain).astype(jnp.bfloat16)

    def mix_block(block_index):
        start_row = (block_index * BLOCK).astype(jnp.int32)
        normed_block = lax.dynamic_slice_in_dim(normed, start_row, BLOCK, 1)
        step_block = lax.dynamic_slice_in_dim(step_sizes, start_row, BLOCK, 1)
        return temporal_mix(normed_block, step_block, decay_rates, skip_gains, state_in_weight, state_out_weight, post_gain)
    mixed_blocks = lax.map(mix_block, jnp.arange(FTOK // BLOCK, dtype=jnp.int32))
    return jnp.transpose(mixed_blocks, (1, 0, 2, 3)).reshape(LATENT_FRAMES, FTOK, SHARED_HEADS * HEAD_DIM)
```

```python
import functools
import math

import jax
import jax.numpy as jnp
from jax import lax
from jax.experimental import pallas as pl
from jax.experimental.pallas import tpu as pltpu
from jax.sharding import PartitionSpec as P

SHARED_HEADS = 16
HEAD_DIM = 128
BLOCK = 128
GROUPS = 4
MESH = pl.DeviceIdType.MESH
F32 = jnp.float32
BF16 = jnp.bfloat16


def remote(src, dst, send_sem, recv_sem, axis, index):
    return pltpu.make_async_remote_copy(
        src_ref=src,
        dst_ref=dst,
        send_sem=send_sem,
        recv_sem=recv_sem,
        device_id={axis: index},
        device_id_type=MESH,
    )


def kernel(
    dims,
    lists_ref,
    rates_ref,
    skips_ref,
    q_ref,
    k_ref,
    v_ref,
    steps_ref,
    pre_ref,
    w_in_ref,
    w_out_ref,
    post_ref,
    out_ref,
    kv_buf,
    a_buf,
    x_buf,
    n_buf,
    y_buf,
    o_buf,
    d_buf,
    own_sem,
    kv_send,
    kv_recv,
    relay_send,
    relay_recv,
    a_send,
    a_recv,
    o_send,
    o_recv,
    self_sem,
):
    space_count, tm_count, list_width = dims
    tokens, channels = q_ref.shape
    rows = tokens // tm_count
    width = channels // GROUPS
    heads_here = width // HEAD_DIM
    chips = space_count // 2
    space = lax.axis_index("space")
    tm = lax.axis_index("tm")
    chip = space // 2
    core = space % 2
    partner = chip * 2 + 1 - core

    barrier = pltpu.get_barrier_semaphore()

    def greet_chip(step, carry):
        peer = lax.rem(chip + step, chips) * 2 + core
        pl.semaphore_signal(barrier, inc=1, device_id={"space": peer}, device_id_type=MESH)
        return carry

    def greet_frame(step, carry):
        peer = lax.rem(tm + step, tm_count)
        pl.semaphore_signal(barrier, inc=1, device_id={"tm": peer}, device_id_type=MESH)
        return carry

    pl.semaphore_signal(barrier, inc=1, device_id={"space": partner}, device_id_type=MESH)
    lax.fori_loop(1, chips, greet_chip, 0)
    lax.fori_loop(1, tm_count, greet_frame, 0)

    def own_copy(which, group):
        source = (k_ref, v_ref)[which]
        return pltpu.make_async_copy(
            source.at[:, pl.ds(group * width, width)],
            kv_buf.at[which, group, space],
            own_sem.at[which, group],
        )

    for group in range(GROUPS):
        for which in range(2):
            own_copy(which, group).start()

    pl.semaphore_wait(barrier, chips + tm_count - 1)

    def direct(which, group, step):
        peer = lax.rem(chip + step, chips) * 2 + core
        source = (k_ref, v_ref)[which]
        return remote(
            source.at[:, pl.ds(group * width, width)],
            kv_buf.at[which, group, space],
            kv_send.at[which, group, step],
            kv_recv.at[which, group, step],
            "space",
            peer,
        )

    def direct_in(which, group, step):
        sender = lax.rem(chip - step + chips, chips) * 2 + core
        return remote(
            kv_buf.at[which, group, sender],
            kv_buf.at[which, group, sender],
            kv_send.at[which, group, step],
            kv_recv.at[which, group, step],
            "space",
            partner,
        )

    def to_partner(which, group, step):
        slot = lax.rem(chip - step + chips, chips) * 2 + core
        return remote(
            kv_buf.at[which, group, slot],
            kv_buf.at[which, group, slot],
            relay_send.at[which, group, step],
            relay_recv.at[which, group, step],
            "space",
            partner,
        )

    def from_partner(which, group, step):
        slot = lax.rem(chip - step + chips, chips) * 2 + 1 - core
        return remote(
            kv_buf.at[which, group, slot],
            kv_buf.at[which, group, slot],
            relay_send.at[which, group, step],
            relay_recv.at[which, group, step],
            "space",
            partner,
        )

    for group in range(GROUPS):
        for which in range(2):

            def send_chip(step, carry):
                direct(which, group, step).start()
                return carry

            lax.fori_loop(1, chips, send_chip, 0)
    for group in range(GROUPS):
        for which in range(2):
            own_copy(which, group).wait()
            to_partner(which, group, 0).start()

    size = tm_count * rows
    row = lax.broadcasted_iota(jnp.int32, (size, size), 0)
    col = lax.broadcasted_iota(jnp.int32, (size, size), 1)
    same = (row % rows == col % rows) & (col // rows <= row // rows)
    lower = same.astype(F32)
    steps = steps_ref[...]
    steps_t = jnp.transpose(steps)
    high = lax.Precision.HIGHEST
    total_rows = lax.dot_general(
        lower, steps, (((1,), (0,)), ((), ())), precision=high, preferred_element_type=F32
    )
    total_cols = lax.dot_general(
        steps_t, lower, (((1,), (1,)), ((), ())), precision=high, preferred_element_type=F32
    )
    for head in range(SHARED_HEADS):
        gap = total_cols[head : head + 1, :] - total_rows[:, head : head + 1]
        decay = jnp.exp(jnp.where(same, gap * rates_ref[head], -1e30))
        d_buf[head] = decay * steps_t[head : head + 1, :]

    block_of = lax.broadcasted_iota(jnp.int32, (1, space_count * tokens), 1) // tokens
    chosen = block_of == lists_ref[space, 0]
    for place in range(1, list_width):
        chosen = chosen | (block_of == lists_ref[space, place])
    bias = jnp.where(chosen, 0.0, -1e30).astype(F32)
    factor = math.log2(math.e) / math.sqrt(HEAD_DIM)

    def frame_out(group, step):
        peer = lax.rem(tm + step, tm_count)
        return remote(
            a_buf.at[group, peer],
            x_buf.at[group, tm],
            a_send.at[group, step],
            a_recv.at[group, step],
            "tm",
            peer,
        )

    def frame_in(group, step):
        sender = lax.rem(tm - step + tm_count, tm_count)
        return remote(
            a_buf.at[group, sender],
            x_buf.at[group, sender],
            a_send.at[group, step],
            a_recv.at[group, step],
            "tm",
            sender,
        )

    def own_frame(group):
        return pltpu.make_async_copy(
            a_buf.at[group, tm], x_buf.at[group, tm], self_sem.at[group]
        )

    for group in range(GROUPS):

        def relay(step, carry):
            for which in range(2):
                direct_in(which, group, step).wait_recv()
                to_partner(which, group, step).start()
            return carry

        def relayed(step, carry):
            for which in range(2):
                from_partner(which, group, step).wait_recv()
            return carry

        lax.fori_loop(1, chips, relay, 0)
        lax.fori_loop(0, chips, relayed, 0)
        for local in range(heads_here):
            lanes = slice(local * HEAD_DIM, (local + 1) * HEAD_DIM)
            head = group * heads_here + local
            query = q_ref[:, head * HEAD_DIM : (head + 1) * HEAD_DIM]
            key = kv_buf[0, group, :, :, lanes].reshape(space_count * tokens, HEAD_DIM)
            value = kv_buf[1, group, :, :, lanes].reshape(space_count * tokens, HEAD_DIM)
            scores = (
                lax.dot_general(
                    query, key, (((1,), (1,)), ((), ())), preferred_element_type=F32
                )
                * factor
                + bias
            )
            weights = jnp.exp2(scores - jnp.max(scores, axis=-1, keepdims=True))
            totals = jnp.sum(weights, axis=-1, keepdims=True)
            summed = jnp.dot(weights.astype(BF16), value, preferred_element_type=F32)
            attended = (summed / totals).reshape(tm_count, rows, HEAD_DIM)
            a_buf[group, :, :, lanes] = attended.astype(BF16)

        def send_frame(step, carry):
            frame_out(group, step).start()
            return carry

        lax.fori_loop(1, tm_count, send_frame, 0)
        own_frame(group).start()

    squares = jnp.zeros((size, 1), F32)
    for group in range(GROUPS):

        def take_frame(step, carry):
            frame_in(group, step).wait_recv()
            return carry

        lax.fori_loop(1, tm_count, take_frame, 0)
        own_frame(group).wait()
        part = x_buf[group].astype(F32).reshape(size, width)
        squares = squares + jnp.sum(part * part, axis=-1, keepdims=True)
    scale = lax.rsqrt(squares / channels + 1e-05)
    state = w_in_ref.shape[1]
    b_in = jnp.zeros((size, state), F32)
    c_out = jnp.zeros((size, state), F32)
    for group in range(GROUPS):
        span = slice(group * width, (group + 1) * width)
        part = x_buf[group].astype(F32).reshape(size, width)
        normed = (part * scale * pre_ref[:, span]).astype(BF16)
        n_buf[group] = normed
        b_in = b_in + jnp.dot(normed, w_in_ref[span, :], preferred_element_type=F32)
        c_out = c_out + jnp.dot(normed, w_out_ref[span, :], preferred_element_type=F32)
    gram = lax.dot_general(
        c_out, b_in, (((1,), (1,)), ((), ())), precision=high, preferred_element_type=F32
    )
    squares = jnp.zeros((size, 1), F32)
    for head in range(SHARED_HEADS):
        group, local = head // heads_here, head % heads_here
        lanes = slice(local * HEAD_DIM, (local + 1) * HEAD_DIM)
        values = n_buf[group, :, lanes]
        mixing = (gram * d_buf[head]).astype(BF16)
        mixed = jnp.dot(mixing, values, preferred_element_type=F32)
        mixed = mixed + skips_ref[head] * values.astype(F32)
        y_buf[:, head * HEAD_DIM : (head + 1) * HEAD_DIM] = mixed
        squares = squares + jnp.sum(mixed * mixed, axis=-1, keepdims=True)
    scale = lax.rsqrt(squares / channels + 1e-05)
    result = y_buf[...] * scale * post_ref[...]
    o_buf[...] = result.reshape(tm_count, rows, channels).astype(BF16)

    def result_out(step):
        peer = lax.rem(tm + step, tm_count)
        return remote(
            o_buf.at[peer], out_ref.at[tm], o_send.at[step], o_recv.at[step], "tm", peer
        )

    def result_in(step):
        sender = lax.rem(tm - step + tm_count, tm_count)
        return remote(
            o_buf.at[sender], out_ref.at[sender], o_send.at[step], o_recv.at[step], "tm", sender
        )

    def send_result(step, carry):
        result_out(step).start()
        return carry

    lax.fori_loop(1, tm_count, send_result, 0)
    own_result = pltpu.make_async_copy(o_buf.at[tm], out_ref.at[tm], self_sem.at[GROUPS])
    own_result.start()

    for group in range(GROUPS):

        def sent_chip(step, carry):
            for which in range(2):
                direct(which, group, step).wait_send()
            return carry

        def sent_partner(step, carry):
            for which in range(2):
                to_partner(which, group, step).wait_send()
            return carry

        def sent_frame(step, carry):
            frame_out(group, step).wait_send()
            return carry

        lax.fori_loop(1, chips, sent_chip, 0)
        lax.fori_loop(0, chips, sent_partner, 0)
        lax.fori_loop(1, tm_count, sent_frame, 0)

    def finish(step, carry):
        result_out(step).wait_send()
        result_in(step).wait_recv()
        return carry

    own_result.wait()
    lax.fori_loop(1, tm_count, finish, 0)


def body(
    queries,
    key_vectors,
    value_vectors,
    block_lists,
    step_sizes,
    decay_rates,
    skip_gains,
    pre_gain,
    state_in_weight,
    state_out_weight,
    post_gain,
):
    tokens, channels = queries.shape[1], queries.shape[2]
    space_count = lax.axis_size("space")
    tm_count = lax.axis_size("tm")
    rows = tokens // tm_count
    width = channels // GROUPS
    chips = space_count // 2
    size = tokens
    vmem = pl.BlockSpec(memory_space=pltpu.VMEM)
    smem = pl.BlockSpec(memory_space=pltpu.SMEM)
    hbm = pl.BlockSpec(memory_space=pl.ANY)
    dma = pltpu.SemaphoreType.DMA
    out = pl.pallas_call(
        functools.partial(kernel, (space_count, tm_count, block_lists.shape[1])),
        out_shape=jax.ShapeDtypeStruct((tm_count, rows, channels), BF16),
        in_specs=[smem, smem, smem, vmem, hbm, hbm, vmem, vmem, vmem, vmem, vmem],
        out_specs=hbm,
        scratch_shapes=[
            pltpu.VMEM((2, GROUPS, space_count, tokens, width), BF16),
            pltpu.VMEM((GROUPS, tm_count, rows, width), BF16),
            pltpu.VMEM((GROUPS, tm_count, rows, width), BF16),
            pltpu.VMEM((GROUPS, size, width), BF16),
            pltpu.VMEM((size, channels), F32),
            pltpu.VMEM((tm_count, rows, channels), BF16),
            pltpu.VMEM((SHARED_HEADS, size, size), F32),
            dma((2, GROUPS)),
            dma((2, GROUPS, chips)),
            dma((2, GROUPS, chips)),
            dma((2, GROUPS, chips)),
            dma((2, GROUPS, chips)),
            dma((GROUPS, tm_count)),
            dma((GROUPS, tm_count)),
            dma((tm_count,)),
            dma((tm_count,)),
            dma((GROUPS + 1,)),
        ],
        compiler_params=pltpu.CompilerParams(
            collective_id=0, has_side_effects=True, vmem_limit_bytes=50 * 1024 * 1024
        ),
        name="attend_and_mix",
    )(
        block_lists,
        decay_rates,
        skip_gains,
        queries.reshape(tokens, channels),
        key_vectors.reshape(tokens, channels),
        value_vectors.reshape(tokens, channels),
        step_sizes.reshape(size, SHARED_HEADS),
        pre_gain.reshape(1, channels),
        state_in_weight,
        state_out_weight,
        post_gain.reshape(1, channels),
    )
    return out.reshape(1, tokens, channels)


def solution(mesh):
    placed = (
        P("tm", "space", None),
        P("tm", "space", None),
        P("tm", "space", None),
        P(),
        P(None, ("space", "tm"), None),
        P(),
        P(),
        P(),
        P(),
        P(),
        P(),
    )
    return jax.shard_map(
        body, mesh=mesh, in_specs=placed, out_specs=P("tm", "space", None), check_vma=False
    )
```

```python
import functools
import math

import jax
import jax.numpy as jnp
from jax import lax
from jax.experimental import pallas as pl
from jax.experimental.pallas import tpu as pltpu
from jax.sharding import PartitionSpec as P

SHARED_HEADS = 16
HEAD_DIM = 128
BLOCK = 128
GROUPS = 4
VMEM_BYTES = 63 * 1024 * 1024
MESH = pl.DeviceIdType.MESH
F32 = jnp.float32
BF16 = jnp.bfloat16


def remote(src, dst, send_sem, recv_sem, axis, index):
    return pltpu.make_async_remote_copy(
        src_ref=src,
        dst_ref=dst,
        send_sem=send_sem,
        recv_sem=recv_sem,
        device_id={axis: index},
        device_id_type=MESH,
    )


def kernel(
    dims,
    lists_hbm,
    rates_hbm,
    skips_hbm,
    q_hbm,
    k_ref,
    v_ref,
    steps_hbm,
    pre_hbm,
    w_in_hbm,
    w_out_hbm,
    post_hbm,
    out_ref,
    lists_ref,
    rates_ref,
    skips_ref,
    q_ref,
    steps_ref,
    pre_ref,
    w_in_ref,
    w_out_ref,
    post_ref,
    load_sem,
    kv_buf,
    a_buf,
    x_buf,
    n_buf,
    y_buf,
    o_buf,
    d_buf,
    own_sem,
    kv_send,
    kv_recv,
    relay_send,
    relay_recv,
    a_send,
    a_recv,
    o_send,
    o_recv,
    self_sem,
):
    space_count, tm_count, list_width = dims
    tokens, channels = q_hbm.shape
    rows = tokens // tm_count
    width = channels // GROUPS
    heads_here = width // HEAD_DIM
    chips = space_count // 2
    space = lax.axis_index("space")
    tm = lax.axis_index("tm")
    chip = space // 2
    core = space % 2
    partner = chip * 2 + 1 - core

    barrier = pltpu.get_barrier_semaphore()

    def greet_chip(step, carry):
        peer = lax.rem(chip + step, chips) * 2 + core
        pl.semaphore_signal(barrier, inc=1, device_id={"space": peer}, device_id_type=MESH)
        return carry

    def greet_frame(step, carry):
        peer = lax.rem(tm + step, tm_count)
        pl.semaphore_signal(barrier, inc=1, device_id={"tm": peer}, device_id_type=MESH)
        return carry

    pl.semaphore_signal(barrier, inc=1, device_id={"space": partner}, device_id_type=MESH)
    lax.fori_loop(1, chips, greet_chip, 0)
    lax.fori_loop(1, tm_count, greet_frame, 0)

    def own_copy(which, group):
        source = (k_ref, v_ref)[which]
        return pltpu.make_async_copy(
            source.at[:, pl.ds(group * width, width)],
            kv_buf.at[which, group, space],
            own_sem.at[which, group],
        )

    for group in range(GROUPS):
        for which in range(2):
            own_copy(which, group).start()

    loads = [
        pltpu.make_async_copy(source, target, load_sem.at[place])
        for place, (source, target) in enumerate(
            (
                (steps_hbm, steps_ref),
                (rates_hbm, rates_ref),
                (lists_hbm, lists_ref),
                (q_hbm, q_ref),
                (skips_hbm, skips_ref),
                (pre_hbm, pre_ref),
                (w_in_hbm, w_in_ref),
                (w_out_hbm, w_out_ref),
                (post_hbm, post_ref),
            )
        )
    ]
    for load in loads:
        load.start()

    pl.semaphore_wait(barrier, chips + tm_count - 1)

    def direct(which, group, step):
        peer = lax.rem(chip + step, chips) * 2 + core
        source = (k_ref, v_ref)[which]
        return remote(
            source.at[:, pl.ds(group * width, width)],
            kv_buf.at[which, group, space],
            kv_send.at[which, group, step],
            kv_recv.at[which, group, step],
            "space",
            peer,
        )

    def direct_in(which, group, step):
        sender = lax.rem(chip - step + chips, chips) * 2 + core
        return remote(
            kv_buf.at[which, group, sender],
            kv_buf.at[which, group, sender],
            kv_send.at[which, group, step],
            kv_recv.at[which, group, step],
            "space",
            partner,
        )

    def to_partner(which, group, step):
        slot = lax.rem(chip - step + chips, chips) * 2 + core
        return remote(
            kv_buf.at[which, group, slot],
            kv_buf.at[which, group, slot],
            relay_send.at[which, group, step],
            relay_recv.at[which, group, step],
            "space",
            partner,
        )

    def from_partner(which, group, step):
        slot = lax.rem(chip - step + chips, chips) * 2 + 1 - core
        return remote(
            kv_buf.at[which, group, slot],
            kv_buf.at[which, group, slot],
            relay_send.at[which, group, step],
            relay_recv.at[which, group, step],
            "space",
            partner,
        )

    for group in range(GROUPS):
        for which in range(2):

            def send_chip(step, carry):
                direct(which, group, step).start()
                return carry

            lax.fori_loop(1, chips, send_chip, 0)
    for group in range(GROUPS):
        for which in range(2):
            own_copy(which, group).wait()
            to_partner(which, group, 0).start()

    for load in loads:
        load.wait()

    size = tm_count * rows
    row = lax.broadcasted_iota(jnp.int32, (size, size), 0)
    col = lax.broadcasted_iota(jnp.int32, (size, size), 1)
    same = (row % rows == col % rows) & (col // rows <= row // rows)
    lower = same.astype(F32)
    steps = steps_ref[...]
    steps_t = jnp.transpose(steps)
    high = lax.Precision.HIGHEST
    total_rows = lax.dot_general(
        lower, steps, (((1,), (0,)), ((), ())), precision=high, preferred_element_type=F32
    )
    total_cols = lax.dot_general(
        steps_t, lower, (((1,), (1,)), ((), ())), precision=high, preferred_element_type=F32
    )
    for head in range(SHARED_HEADS):
        gap = total_cols[head : head + 1, :] - total_rows[:, head : head + 1]
        decay = jnp.exp(jnp.where(same, gap * rates_ref[head], -1e30))
        d_buf[head] = decay * steps_t[head : head + 1, :]

    block_of = lax.broadcasted_iota(jnp.int32, (1, space_count * tokens), 1) // tokens
    chosen = block_of == lists_ref[space, 0]
    for place in range(1, list_width):
        chosen = chosen | (block_of == lists_ref[space, place])
    bias = jnp.where(chosen, 0.0, -1e30).astype(F32)
    factor = math.log2(math.e) / math.sqrt(HEAD_DIM)

    def frame_out(group, step):
        peer = lax.rem(tm + step, tm_count)
        return remote(
            a_buf.at[group, peer],
            x_buf.at[group, tm],
            a_send.at[group, step],
            a_recv.at[group, step],
            "tm",
            peer,
        )

    def frame_in(group, step):
        sender = lax.rem(tm - step + tm_count, tm_count)
        return remote(
            a_buf.at[group, sender],
            x_buf.at[group, sender],
            a_send.at[group, step],
            a_recv.at[group, step],
            "tm",
            sender,
        )

    def own_frame(group):
        return pltpu.make_async_copy(
            a_buf.at[group, tm], x_buf.at[group, tm], self_sem.at[group]
        )

    for group in range(GROUPS):

        def relay(step, carry):
            for which in range(2):
                direct_in(which, group, step).wait_recv()
                to_partner(which, group, step).start()
            return carry

        def relayed(step, carry):
            for which in range(2):
                from_partner(which, group, step).wait_recv()
            return carry

        lax.fori_loop(1, chips, relay, 0)
        lax.fori_loop(0, chips, relayed, 0)
        for local in range(heads_here):
            lanes = slice(local * HEAD_DIM, (local + 1) * HEAD_DIM)
            head = group * heads_here + local
            query = q_ref[:, head * HEAD_DIM : (head + 1) * HEAD_DIM]
            key = kv_buf[0, group, :, :, lanes].reshape(space_count * tokens, HEAD_DIM)
            value = kv_buf[1, group, :, :, lanes].reshape(space_count * tokens, HEAD_DIM)
            scores = (
                lax.dot_general(
                    query, key, (((1,), (1,)), ((), ())), preferred_element_type=F32
                )
                * factor
                + bias
            )
            weights = jnp.exp2(scores - jnp.max(scores, axis=-1, keepdims=True))
            totals = jnp.sum(weights, axis=-1, keepdims=True)
            summed = jnp.dot(weights.astype(BF16), value, preferred_element_type=F32)
            attended = (summed / totals).reshape(tm_count, rows, HEAD_DIM)
            a_buf[group, :, :, lanes] = attended.astype(BF16)

        def send_frame(step, carry):
            frame_out(group, step).start()
            return carry

        lax.fori_loop(1, tm_count, send_frame, 0)
        own_frame(group).start()

    squares = jnp.zeros((size, 1), F32)
    for group in range(GROUPS):

        def take_frame(step, carry):
            frame_in(group, step).wait_recv()
            return carry

        lax.fori_loop(1, tm_count, take_frame, 0)
        own_frame(group).wait()
        part = x_buf[group].astype(F32).reshape(size, width)
        squares = squares + jnp.sum(part * part, axis=-1, keepdims=True)
    scale = lax.rsqrt(squares / channels + 1e-05)
    state = w_in_ref.shape[0]
    b_in = jnp.zeros((size, state), F32)
    c_out = jnp.zeros((size, state), F32)
    for group in range(GROUPS):
        span = slice(group * width, (group + 1) * width)
        part = x_buf[group].astype(F32).reshape(size, width)
        normed = (part * scale * pre_ref[:, span]).astype(BF16)
        n_buf[group] = normed
        across = (((1,), (1,)), ((), ()))
        b_in = b_in + lax.dot_general(
            normed, w_in_ref[:, span], across, preferred_element_type=F32
        )
        c_out = c_out + lax.dot_general(
            normed, w_out_ref[:, span], across, preferred_element_type=F32
        )
    gram = lax.dot_general(
        c_out, b_in, (((1,), (1,)), ((), ())), precision=high, preferred_element_type=F32
    )
    squares = jnp.zeros((size, 1), F32)
    for head in range(SHARED_HEADS):
        group, local = head // heads_here, head % heads_here
        lanes = slice(local * HEAD_DIM, (local + 1) * HEAD_DIM)
        values = n_buf[group, :, lanes]
        mixing = (gram * d_buf[head]).astype(BF16)
        mixed = jnp.dot(mixing, values, preferred_element_type=F32)
        mixed = mixed + skips_ref[head] * values.astype(F32)
        y_buf[:, head * HEAD_DIM : (head + 1) * HEAD_DIM] = mixed
        squares = squares + jnp.sum(mixed * mixed, axis=-1, keepdims=True)
    scale = lax.rsqrt(squares / channels + 1e-05)
    result = y_buf[...] * scale * post_ref[...]
    o_buf[...] = result.reshape(tm_count, rows, channels).astype(BF16)

    def result_out(step):
        peer = lax.rem(tm + step, tm_count)
        return remote(
            o_buf.at[peer], out_ref.at[tm], o_send.at[step], o_recv.at[step], "tm", peer
        )

    def result_in(step):
        sender = lax.rem(tm - step + tm_count, tm_count)
        return remote(
            o_buf.at[sender], out_ref.at[sender], o_send.at[step], o_recv.at[step], "tm", sender
        )

    def send_result(step, carry):
        result_out(step).start()
        return carry

    lax.fori_loop(1, tm_count, send_result, 0)
    own_result = pltpu.make_async_copy(o_buf.at[tm], out_ref.at[tm], self_sem.at[GROUPS])
    own_result.start()

    for group in range(GROUPS):

        def sent_chip(step, carry):
            for which in range(2):
                direct(which, group, step).wait_send()
            return carry

        def sent_partner(step, carry):
            for which in range(2):
                to_partner(which, group, step).wait_send()
            return carry

        def sent_frame(step, carry):
            frame_out(group, step).wait_send()
            return carry

        lax.fori_loop(1, chips, sent_chip, 0)
        lax.fori_loop(0, chips, sent_partner, 0)
        lax.fori_loop(1, tm_count, sent_frame, 0)

    def finish(step, carry):
        result_out(step).wait_send()
        result_in(step).wait_recv()
        return carry

    own_result.wait()
    lax.fori_loop(1, tm_count, finish, 0)


def body(
    queries,
    key_vectors,
    value_vectors,
    block_lists,
    step_sizes,
    decay_rates,
    skip_gains,
    pre_gain,
    state_in_weight,
    state_out_weight,
    post_gain,
):
    tokens, channels = queries.shape[1], queries.shape[2]
    space_count = lax.axis_size("space")
    tm_count = lax.axis_size("tm")
    rows = tokens // tm_count
    width = channels // GROUPS
    chips = space_count // 2
    size = tokens
    state = state_in_weight.shape[1]
    hbm = pl.BlockSpec(memory_space=pl.ANY)
    dma = pltpu.SemaphoreType.DMA
    out = pl.pallas_call(
        functools.partial(kernel, (space_count, tm_count, block_lists.shape[1])),
        out_shape=jax.ShapeDtypeStruct((tm_count, rows, channels), BF16),
        in_specs=[hbm] * 11,
        out_specs=hbm,
        scratch_shapes=[
            pltpu.SMEM(block_lists.shape, jnp.int32),
            pltpu.SMEM(decay_rates.shape, F32),
            pltpu.SMEM(skip_gains.shape, F32),
            pltpu.VMEM((tokens, channels), BF16),
            pltpu.VMEM((size, SHARED_HEADS), F32),
            pltpu.VMEM((1, channels), F32),
            pltpu.VMEM((state, channels), BF16),
            pltpu.VMEM((state, channels), BF16),
            pltpu.VMEM((1, channels), F32),
            dma((9,)),
            pltpu.VMEM((2, GROUPS, space_count, tokens, width), BF16),
            pltpu.VMEM((GROUPS, tm_count, rows, width), BF16),
            pltpu.VMEM((GROUPS, tm_count, rows, width), BF16),
            pltpu.VMEM((GROUPS, size, width), BF16),
            pltpu.VMEM((size, channels), F32),
            pltpu.VMEM((tm_count, rows, channels), BF16),
            pltpu.VMEM((SHARED_HEADS, size, size), F32),
            dma((2, GROUPS)),
            dma((2, GROUPS, chips)),
            dma((2, GROUPS, chips)),
            dma((2, GROUPS, chips)),
            dma((2, GROUPS, chips)),
            dma((GROUPS, tm_count)),
            dma((GROUPS, tm_count)),
            dma((tm_count,)),
            dma((tm_count,)),
            dma((GROUPS + 1,)),
        ],
        compiler_params=pltpu.CompilerParams(
            collective_id=0, has_side_effects=True, vmem_limit_bytes=VMEM_BYTES
        ),
        name="attend_and_mix",
    )(
        block_lists,
        decay_rates,
        skip_gains,
        queries.reshape(tokens, channels),
        key_vectors.reshape(tokens, channels),
        value_vectors.reshape(tokens, channels),
        step_sizes.reshape(size, SHARED_HEADS),
        pre_gain.reshape(1, channels),
        state_in_weight.T,
        state_out_weight.T,
        post_gain.reshape(1, channels),
    )
    return out.reshape(1, tokens, channels)


def solution(mesh):
    placed = (
        P("tm", "space", None),
        P("tm", "space", None),
        P("tm", "space", None),
        P(),
        P(None, ("space", "tm"), None),
        P(),
        P(),
        P(),
        P(),
        P(),
        P(),
    )
    return jax.shard_map(
        body, mesh=mesh, in_specs=placed, out_specs=P("tm", "space", None), check_vma=False
    )
```

```python
import functools
import math

import jax
import jax.numpy as jnp
from jax import lax
from jax.experimental import pallas as pl
from jax.experimental.pallas import tpu as pltpu
from jax.sharding import PartitionSpec as P

SHARED_HEADS = 16
HEAD_DIM = 128
BLOCK = 128
GROUPS = 8
VMEM_BYTES = 63 * 1024 * 1024
MESH = pl.DeviceIdType.MESH
F32 = jnp.float32
BF16 = jnp.bfloat16


def remote(src, dst, send_sem, recv_sem, axis, index):
    return pltpu.make_async_remote_copy(
        src_ref=src,
        dst_ref=dst,
        send_sem=send_sem,
        recv_sem=recv_sem,
        device_id={axis: index},
        device_id_type=MESH,
    )


def kernel(
    dims,
    lists_hbm,
    rates_hbm,
    skips_hbm,
    q_hbm,
    k_ref,
    v_ref,
    steps_hbm,
    pre_hbm,
    w_in_hbm,
    w_out_hbm,
    post_hbm,
    out_ref,
    lists_ref,
    rates_ref,
    skips_ref,
    q_ref,
    steps_ref,
    pre_ref,
    w_in_ref,
    w_out_ref,
    post_ref,
    load_sem,
    step_send,
    step_recv,
    step_own,
    kv_buf,
    a_buf,
    x_buf,
    n_buf,
    y_buf,
    o_buf,
    d_buf,
    own_sem,
    kv_send,
    kv_recv,
    relay_send,
    relay_recv,
    a_send,
    a_recv,
    l_send,
    l_recv,
    o_send,
    o_recv,
    self_sem,
):
    space_count, tm_count, list_width = dims
    tokens, channels = q_hbm.shape
    half_count = tm_count // 2
    rows = tokens // half_count
    width = channels // GROUPS
    heads_here = width // HEAD_DIM
    chips = space_count // 2
    space = lax.axis_index("space")
    tm = lax.axis_index("tm")
    half = tm // half_count
    place = tm % half_count
    chip = space // 2
    core = space % 2
    partner = chip * 2 + 1 - core

    barrier = pltpu.get_barrier_semaphore()

    def greet_chip(step, carry):
        peer = lax.rem(chip + step, chips) * 2 + core
        pl.semaphore_signal(barrier, inc=1, device_id={"space": peer}, device_id_type=MESH)
        return carry

    def greet_frame(step, carry):
        peer = lax.rem(tm + step, tm_count)
        pl.semaphore_signal(barrier, inc=1, device_id={"tm": peer}, device_id_type=MESH)
        return carry

    pl.semaphore_signal(barrier, inc=1, device_id={"space": partner}, device_id_type=MESH)
    lax.fori_loop(1, chips, greet_chip, 0)
    lax.fori_loop(1, tm_count, greet_frame, 0)

    def own_copy(which, group):
        source = (k_ref, v_ref)[which]
        return pltpu.make_async_copy(
            source.at[:, pl.ds(group * width, width)],
            kv_buf.at[which, group, space],
            own_sem.at[which, group],
        )

    for group in range(GROUPS):
        for which in range(2):
            own_copy(which, group).start()

    loads = [
        pltpu.make_async_copy(source, target, load_sem.at[index])
        for index, (source, target) in enumerate(
            (
                (rates_hbm, rates_ref),
                (lists_hbm, lists_ref),
                (q_hbm, q_ref),
                (skips_hbm, skips_ref),
                (pre_hbm, pre_ref),
                (w_in_hbm, w_in_ref),
                (w_out_hbm, w_out_ref),
                (post_hbm, post_ref),
            )
        )
    ]
    for load in loads:
        load.start()

    pl.semaphore_wait(barrier, chips + tm_count - 1)

    def direct(which, group, step):
        peer = lax.rem(chip + step, chips) * 2 + core
        source = (k_ref, v_ref)[which]
        return remote(
            source.at[:, pl.ds(group * width, width)],
            kv_buf.at[which, group, space],
            kv_send.at[which, group, step],
            kv_recv.at[which, group, step],
            "space",
            peer,
        )

    def direct_in(which, group, step):
        sender = lax.rem(chip - step + chips, chips) * 2 + core
        return remote(
            kv_buf.at[which, group, sender],
            kv_buf.at[which, group, sender],
            kv_send.at[which, group, step],
            kv_recv.at[which, group, step],
            "space",
            partner,
        )

    def to_partner(which, group, step):
        slot = lax.rem(chip - step + chips, chips) * 2 + core
        return remote(
            kv_buf.at[which, group, slot],
            kv_buf.at[which, group, slot],
            relay_send.at[which, group, step],
            relay_recv.at[which, group, step],
            "space",
            partner,
        )

    def from_partner(which, group, step):
        slot = lax.rem(chip - step + chips, chips) * 2 + 1 - core
        return remote(
            kv_buf.at[which, group, slot],
            kv_buf.at[which, group, slot],
            relay_send.at[which, group, step],
            relay_recv.at[which, group, step],
            "space",
            partner,
        )

    def step_copy(which, target, part):
        return remote(
            steps_hbm,
            steps_ref.at[:, part],
            step_send.at[which],
            step_recv.at[part],
            "tm",
            target,
        )

    def step_arrival(part, origin):
        return remote(
            steps_hbm,
            steps_ref.at[:, part],
            step_send.at[0],
            step_recv.at[part],
            "tm",
            origin,
        )

    def step_local(part):
        return pltpu.make_async_copy(steps_hbm, steps_ref.at[:, part], step_own.at[part])

    for group in range(GROUPS):
        for which in range(2):

            def send_chip(step, carry):
                direct(which, group, step).start()
                return carry

            lax.fori_loop(1, chips, send_chip, 0)
    for group in range(GROUPS):
        for which in range(2):
            own_copy(which, group).wait()
            to_partner(which, group, 0).start()

    for which in range(2):
        target = which * half_count + tm // 2
        part = tm % 2

        @pl.when(target != tm)
        def _():
            step_copy(which, target, part).start()

        @pl.when(target == tm)
        def _():
            step_local(part).start()

    for load in loads:
        load.wait()
    for part in range(2):
        origin = 2 * place + part

        @pl.when(origin != tm)
        def _():
            step_arrival(part, origin).wait_recv()

        @pl.when(origin == tm)
        def _():
            step_local(part).wait()

    size = half_count * rows
    row = lax.broadcasted_iota(jnp.int32, (2 * size, 2 * size), 0)
    col = lax.broadcasted_iota(jnp.int32, (2 * size, 2 * size), 1)
    same = (row % rows == col % rows) & (col // rows <= row // rows)
    lower = same.astype(F32)
    steps = steps_ref[...].reshape(2 * size, SHARED_HEADS)
    swapped = jnp.concatenate([steps[size:], steps[:size]], axis=0)
    steps = jnp.where(half == 1, steps, swapped)
    steps_t = jnp.transpose(steps)
    high = lax.Precision.HIGHEST
    total_rows = lax.dot_general(
        lower[size:], steps, (((1,), (0,)), ((), ())), precision=high, preferred_element_type=F32
    )
    total_cols = lax.dot_general(
        steps_t, lower, (((1,), (1,)), ((), ())), precision=high, preferred_element_type=F32
    )
    first = (1 - half) * size
    counts = (lower[size:] > 0.5) & (col[size:] >= first)
    for head in range(SHARED_HEADS):
        gap = total_cols[head : head + 1, :] - total_rows[:, head : head + 1]
        decay = jnp.exp(jnp.where(counts, gap * rates_ref[head], -1e30))
        d_buf[head] = decay * steps_t[head : head + 1, :]

    @pl.when(half == 0)
    def _():
        x_buf[:, 0:half_count] = jnp.zeros((GROUPS, half_count, rows, width), BF16)

    block_of = lax.broadcasted_iota(jnp.int32, (1, space_count * tokens), 1) // tokens
    chosen = block_of == lists_ref[space, 0]
    for entry in range(1, list_width):
        chosen = chosen | (block_of == lists_ref[space, entry])
    bias = jnp.where(chosen, 0.0, -1e30).astype(F32)
    factor = math.log2(math.e) / math.sqrt(HEAD_DIM)

    def frame_out(group, step):
        peer = lax.rem(place + step, half_count)
        return remote(
            a_buf.at[group, peer],
            x_buf.at[group, half_count + place],
            a_send.at[group, step],
            a_recv.at[group, step],
            "tm",
            half * half_count + peer,
        )

    def frame_in(group, step):
        sender = lax.rem(place - step + half_count, half_count)
        return remote(
            a_buf.at[group, sender],
            x_buf.at[group, half_count + sender],
            a_send.at[group, step],
            a_recv.at[group, step],
            "tm",
            half * half_count + sender,
        )

    def later_out(group, step):
        peer = lax.rem(place + step, half_count)
        return remote(
            a_buf.at[group, peer],
            x_buf.at[group, place],
            l_send.at[group, step],
            l_recv.at[group, step],
            "tm",
            half_count + peer,
        )

    def earlier_in(group, step):
        sender = lax.rem(place - step + half_count, half_count)
        return remote(
            a_buf.at[group, sender],
            x_buf.at[group, sender],
            l_send.at[group, step],
            l_recv.at[group, step],
            "tm",
            sender,
        )

    def own_frame(group):
        return pltpu.make_async_copy(
            a_buf.at[group, place], x_buf.at[group, half_count + place], self_sem.at[group]
        )

    for group in range(GROUPS):

        def relay(step, carry):
            for which in range(2):
                direct_in(which, group, step).wait_recv()
                to_partner(which, group, step).start()
            return carry

        def relayed(step, carry):
            for which in range(2):
                from_partner(which, group, step).wait_recv()
            return carry

        lax.fori_loop(1, chips, relay, 0)
        lax.fori_loop(0, chips, relayed, 0)
        for local in range(heads_here):
            lanes = slice(local * HEAD_DIM, (local + 1) * HEAD_DIM)
            head = group * heads_here + local
            query = q_ref[:, head * HEAD_DIM : (head + 1) * HEAD_DIM]
            key = kv_buf[0, group, :, :, lanes].reshape(space_count * tokens, HEAD_DIM)
            value = kv_buf[1, group, :, :, lanes].reshape(space_count * tokens, HEAD_DIM)
            scores = (
                lax.dot_general(
                    query, key, (((1,), (1,)), ((), ())), preferred_element_type=F32
                )
                * factor
                + bias
            )
            weights = jnp.exp2(scores - jnp.max(scores, axis=-1, keepdims=True))
            totals = jnp.sum(weights, axis=-1, keepdims=True)
            summed = jnp.dot(weights.astype(BF16), value, preferred_element_type=F32)
            attended = (summed / totals).reshape(half_count, rows, HEAD_DIM)
            a_buf[group, :, :, lanes] = attended.astype(BF16)

        def send_frame(step, carry):
            frame_out(group, step).start()
            return carry

        def send_later(step, carry):
            later_out(group, step).start()
            return carry

        @pl.when(half == 0)
        def _():
            lax.fori_loop(0, half_count, send_later, 0)

        lax.fori_loop(1, half_count, send_frame, 0)
        own_frame(group).start()

    squares = jnp.zeros((2 * size, 1), F32)
    for group in range(GROUPS):

        def take_frame(step, carry):
            frame_in(group, step).wait_recv()
            return carry

        def take_earlier(step, carry):
            earlier_in(group, step).wait_recv()
            return carry

        lax.fori_loop(1, half_count, take_frame, 0)
        own_frame(group).wait()

        @pl.when(half == 1)
        def _():
            lax.fori_loop(0, half_count, take_earlier, 0)

        part = x_buf[group].astype(F32).reshape(2 * size, width)
        squares = squares + jnp.sum(part * part, axis=-1, keepdims=True)
    scale = lax.rsqrt(squares / channels + 1e-05)
    state = w_in_ref.shape[0]
    b_in = jnp.zeros((2 * size, state), F32)
    c_out = jnp.zeros((size, state), F32)
    across = (((1,), (1,)), ((), ()))
    for group in range(GROUPS):
        span = slice(group * width, (group + 1) * width)
        part = x_buf[group].astype(F32).reshape(2 * size, width)
        normed = (part * scale * pre_ref[:, span]).astype(BF16)
        n_buf[group] = normed
        b_in = b_in + lax.dot_general(
            normed, w_in_ref[:, span], across, preferred_element_type=F32
        )
        c_out = c_out + lax.dot_general(
            normed[size:], w_out_ref[:, span], across, preferred_element_type=F32
        )
    gram = lax.dot_general(c_out, b_in, across, precision=high, preferred_element_type=F32)
    squares = jnp.zeros((size, 1), F32)
    for head in range(SHARED_HEADS):
        group, local = head // heads_here, head % heads_here
        lanes = slice(local * HEAD_DIM, (local + 1) * HEAD_DIM)
        values = n_buf[group, :, lanes]
        mixing = (gram * d_buf[head]).astype(BF16)
        mixed = jnp.dot(mixing, values, preferred_element_type=F32)
        mixed = mixed + skips_ref[head] * values[size:].astype(F32)
        y_buf[:, head * HEAD_DIM : (head + 1) * HEAD_DIM] = mixed
        squares = squares + jnp.sum(mixed * mixed, axis=-1, keepdims=True)
    scale = lax.rsqrt(squares / channels + 1e-05)
    result = y_buf[...] * scale * post_ref[...]
    o_buf[...] = result.reshape(half_count, rows, channels).astype(BF16)

    def result_out(step):
        peer = lax.rem(place + step, half_count)
        return remote(
            o_buf.at[peer],
            out_ref.at[place],
            o_send.at[step],
            o_recv.at[step],
            "tm",
            half * half_count + peer,
        )

    def result_in(step):
        sender = lax.rem(place - step + half_count, half_count)
        return remote(
            o_buf.at[sender],
            out_ref.at[sender],
            o_send.at[step],
            o_recv.at[step],
            "tm",
            half * half_count + sender,
        )

    def send_result(step, carry):
        result_out(step).start()
        return carry

    lax.fori_loop(1, half_count, send_result, 0)
    own_result = pltpu.make_async_copy(o_buf.at[place], out_ref.at[place], self_sem.at[GROUPS])
    own_result.start()

    for group in range(GROUPS):

        def sent_chip(step, carry):
            for which in range(2):
                direct(which, group, step).wait_send()
            return carry

        def sent_partner(step, carry):
            for which in range(2):
                to_partner(which, group, step).wait_send()
            return carry

        def sent_frame(step, carry):
            frame_out(group, step).wait_send()
            return carry

        lax.fori_loop(1, chips, sent_chip, 0)
        lax.fori_loop(0, chips, sent_partner, 0)
        lax.fori_loop(1, half_count, sent_frame, 0)

        def sent_later(step, carry):
            later_out(group, step).wait_send()
            return carry

        @pl.when(half == 0)
        def _():
            lax.fori_loop(0, half_count, sent_later, 0)

    for which in range(2):
        target = which * half_count + tm // 2

        @pl.when(target != tm)
        def _():
            step_copy(which, target, tm % 2).wait_send()


    def finish(step, carry):
        result_out(step).wait_send()
        result_in(step).wait_recv()
        return carry

    own_result.wait()
    lax.fori_loop(1, half_count, finish, 0)


def body(
    queries,
    key_vectors,
    value_vectors,
    block_lists,
    step_sizes,
    decay_rates,
    skip_gains,
    pre_gain,
    state_in_weight,
    state_out_weight,
    post_gain,
):
    tokens, channels = queries.shape[1], queries.shape[2]
    space_count = lax.axis_size("space")
    tm_count = lax.axis_size("tm")
    half_count = tm_count // 2
    rows = tokens // half_count
    width = channels // GROUPS
    chips = space_count // 2
    size = tokens
    state = state_in_weight.shape[1]
    hbm = pl.BlockSpec(memory_space=pl.ANY)
    dma = pltpu.SemaphoreType.DMA
    out = pl.pallas_call(
        functools.partial(kernel, (space_count, tm_count, block_lists.shape[1])),
        out_shape=jax.ShapeDtypeStruct((half_count, rows, channels), BF16),
        in_specs=[hbm] * 11,
        out_specs=hbm,
        scratch_shapes=[
            pltpu.SMEM(block_lists.shape, jnp.int32),
            pltpu.SMEM(decay_rates.shape, F32),
            pltpu.SMEM(skip_gains.shape, F32),
            pltpu.VMEM((tokens, channels), BF16),
            pltpu.VMEM((tm_count, 2, tokens // tm_count, SHARED_HEADS), F32),
            pltpu.VMEM((1, channels), F32),
            pltpu.VMEM((state, channels), BF16),
            pltpu.VMEM((state, channels), BF16),
            pltpu.VMEM((1, channels), F32),
            dma((8,)),
            dma((2,)),
            dma((2,)),
            dma((2,)),
            pltpu.VMEM((2, GROUPS, space_count, tokens, width), BF16),
            pltpu.VMEM((GROUPS, half_count, rows, width), BF16),
            pltpu.VMEM((GROUPS, tm_count, rows, width), BF16),
            pltpu.VMEM((GROUPS, 2 * size, width), BF16),
            pltpu.VMEM((size, channels), F32),
            pltpu.VMEM((half_count, rows, channels), BF16),
            pltpu.VMEM((SHARED_HEADS, size, 2 * size), F32),
            dma((2, GROUPS)),
            dma((2, GROUPS, chips)),
            dma((2, GROUPS, chips)),
            dma((2, GROUPS, chips)),
            dma((2, GROUPS, chips)),
            dma((GROUPS, half_count)),
            dma((GROUPS, half_count)),
            dma((GROUPS, half_count)),
            dma((GROUPS, half_count)),
            dma((half_count,)),
            dma((half_count,)),
            dma((GROUPS + 1,)),
        ],
        compiler_params=pltpu.CompilerParams(
            collective_id=0, has_side_effects=True, vmem_limit_bytes=VMEM_BYTES
        ),
        name="attend_and_mix",
    )(
        block_lists,
        decay_rates,
        skip_gains,
        queries.reshape(tokens, channels),
        key_vectors.reshape(tokens, channels),
        value_vectors.reshape(tokens, channels),
        step_sizes,
        pre_gain.reshape(1, channels),
        state_in_weight.T,
        state_out_weight.T,
        post_gain.reshape(1, channels),
    )
    return out.reshape(1, tokens, channels)


def solution(mesh):
    placed = (
        P("tm", "space", None),
        P("tm", "space", None),
        P("tm", "space", None),
        P(),
        P(None, ("space", "tm"), None),
        P(),
        P(),
        P(),
        P(),
        P(),
        P(),
    )
    return jax.shard_map(
        body, mesh=mesh, in_specs=placed, out_specs=P("tm", "space", None), check_vma=False
    )
```

```python
import functools
import math

import jax
import jax.numpy as jnp
from jax import lax
from jax.experimental import pallas as pl
from jax.experimental.pallas import tpu as pltpu
from jax.sharding import PartitionSpec as P

SHARED_HEADS = 16
HEAD_DIM = 128
BLOCK = 128
GROUPS = 8
LAG = 3
VMEM_BYTES = 63 * 1024 * 1024
MESH = pl.DeviceIdType.MESH
F32 = jnp.float32
BF16 = jnp.bfloat16


def remote(src, dst, send_sem, recv_sem, axis, index):
    return pltpu.make_async_remote_copy(
        src_ref=src,
        dst_ref=dst,
        send_sem=send_sem,
        recv_sem=recv_sem,
        device_id={axis: index},
        device_id_type=MESH,
    )


def kernel(
    dims,
    lists_hbm,
    rates_hbm,
    skips_hbm,
    q_hbm,
    k_ref,
    v_ref,
    steps_hbm,
    pre_hbm,
    w_in_hbm,
    w_out_hbm,
    post_hbm,
    out_ref,
    lists_ref,
    rates_ref,
    skips_ref,
    q_ref,
    steps_ref,
    pre_ref,
    w_in_ref,
    w_out_ref,
    post_ref,
    load_sem,
    step_send,
    step_recv,
    step_own,
    kv_buf,
    a_buf,
    x_buf,
    n_buf,
    y_buf,
    o_buf,
    d_buf,
    own_sem,
    kv_send,
    kv_recv,
    relay_send,
    relay_recv,
    a_send,
    a_recv,
    l_send,
    l_recv,
    o_send,
    o_recv,
    self_sem,
):
    space_count, tm_count, list_width = dims
    tokens, channels = q_hbm.shape
    half_count = tm_count // 2
    rows = tokens // half_count
    width = channels // GROUPS
    heads_here = width // HEAD_DIM
    chips = space_count // 2
    space = lax.axis_index("space")
    tm = lax.axis_index("tm")
    half = tm // half_count
    place = tm % half_count
    chip = space // 2
    core = space % 2
    partner = chip * 2 + 1 - core

    barrier = pltpu.get_barrier_semaphore()

    def greet_chip(step, carry):
        peer = lax.rem(chip + step, chips) * 2 + core
        pl.semaphore_signal(barrier, inc=1, device_id={"space": peer}, device_id_type=MESH)
        return carry

    def greet_frame(step, carry):
        peer = lax.rem(tm + step, tm_count)
        pl.semaphore_signal(barrier, inc=1, device_id={"tm": peer}, device_id_type=MESH)
        return carry

    pl.semaphore_signal(barrier, inc=1, device_id={"space": partner}, device_id_type=MESH)
    lax.fori_loop(1, chips, greet_chip, 0)
    lax.fori_loop(1, tm_count, greet_frame, 0)

    def own_copy(which, group):
        source = (k_ref, v_ref)[which]
        return pltpu.make_async_copy(
            source.at[:, pl.ds(group * width, width)],
            kv_buf.at[group, space, which],
            own_sem.at[which, group],
        )

    for group in range(GROUPS):
        for which in range(2):
            own_copy(which, group).start()

    loads = [
        pltpu.make_async_copy(source, target, load_sem.at[index])
        for index, (source, target) in enumerate(
            (
                (rates_hbm, rates_ref),
                (lists_hbm, lists_ref),
                (q_hbm, q_ref),
                (skips_hbm, skips_ref),
                (pre_hbm, pre_ref),
                (w_in_hbm, w_in_ref),
                (w_out_hbm, w_out_ref),
                (post_hbm, post_ref),
            )
        )
    ]
    for load in loads:
        load.start()

    pl.semaphore_wait(barrier, chips + tm_count - 1)

    def direct(group, step):
        peer = lax.rem(chip + step, chips) * 2 + core
        return remote(
            kv_buf.at[group, space],
            kv_buf.at[group, space],
            kv_send.at[group, step],
            kv_recv.at[group, step],
            "space",
            peer,
        )

    def direct_in(group, step):
        sender = lax.rem(chip - step + chips, chips) * 2 + core
        return remote(
            kv_buf.at[group, sender],
            kv_buf.at[group, sender],
            kv_send.at[group, step],
            kv_recv.at[group, step],
            "space",
            partner,
        )

    def to_partner(group, step):
        slot = lax.rem(chip - step + chips, chips) * 2 + core
        return remote(
            kv_buf.at[group, slot],
            kv_buf.at[group, slot],
            relay_send.at[group, step],
            relay_recv.at[group, step],
            "space",
            partner,
        )

    def from_partner(group, step):
        slot = lax.rem(chip - step + chips, chips) * 2 + 1 - core
        return remote(
            kv_buf.at[group, slot],
            kv_buf.at[group, slot],
            relay_send.at[group, step],
            relay_recv.at[group, step],
            "space",
            partner,
        )

    def step_copy(which, target, part):
        return remote(
            steps_hbm,
            steps_ref.at[:, part],
            step_send.at[which],
            step_recv.at[part],
            "tm",
            target,
        )

    def step_arrival(part, origin):
        return remote(
            steps_hbm,
            steps_ref.at[:, part],
            step_send.at[0],
            step_recv.at[part],
            "tm",
            origin,
        )

    def step_local(part):
        return pltpu.make_async_copy(steps_hbm, steps_ref.at[:, part], step_own.at[part])

    for group in range(GROUPS):
        for which in range(2):
            own_copy(which, group).wait()

        def send_chip(step, carry):
            direct(group, step).start()
            return carry

        lax.fori_loop(1, chips, send_chip, 0)
    for group in range(GROUPS):
        to_partner(group, 0).start()

    for which in range(2):
        target = which * half_count + tm // 2
        part = tm % 2

        @pl.when(target != tm)
        def _():
            step_copy(which, target, part).start()

        @pl.when(target == tm)
        def _():
            step_local(part).start()

    for load in loads:
        load.wait()
    for part in range(2):
        origin = 2 * place + part

        @pl.when(origin != tm)
        def _():
            step_arrival(part, origin).wait_recv()

        @pl.when(origin == tm)
        def _():
            step_local(part).wait()

    size = half_count * rows
    row = lax.broadcasted_iota(jnp.int32, (2 * size, 2 * size), 0)
    col = lax.broadcasted_iota(jnp.int32, (2 * size, 2 * size), 1)
    same = (row % rows == col % rows) & (col // rows <= row // rows)
    lower = same.astype(F32)
    steps = steps_ref[...].reshape(2 * size, SHARED_HEADS)
    swapped = jnp.concatenate([steps[size:], steps[:size]], axis=0)
    steps = jnp.where(half == 1, steps, swapped)
    steps_t = jnp.transpose(steps)
    high = lax.Precision.HIGHEST
    total_rows = lax.dot_general(
        lower[size:], steps, (((1,), (0,)), ((), ())), precision=high, preferred_element_type=F32
    )
    total_cols = lax.dot_general(
        steps_t, lower, (((1,), (1,)), ((), ())), precision=high, preferred_element_type=F32
    )
    first = (1 - half) * size
    counts = (lower[size:] > 0.5) & (col[size:] >= first)
    for head in range(SHARED_HEADS):
        gap = total_cols[head : head + 1, :] - total_rows[:, head : head + 1]
        decay = jnp.exp(jnp.where(counts, gap * rates_ref[head], -1e30))
        d_buf[head] = decay * steps_t[head : head + 1, :]

    @pl.when(half == 0)
    def _():
        x_buf[:, 0:half_count] = jnp.zeros((GROUPS, half_count, rows, width), BF16)

    block_of = lax.broadcasted_iota(jnp.int32, (1, space_count * tokens), 1) // tokens
    chosen = block_of == lists_ref[space, 0]
    for entry in range(1, list_width):
        chosen = chosen | (block_of == lists_ref[space, entry])
    bias = jnp.where(chosen, 0.0, -1e30).astype(F32)
    factor = math.log2(math.e) / math.sqrt(HEAD_DIM)

    def frame_out(group, step):
        peer = lax.rem(place + step, half_count)
        return remote(
            a_buf.at[group, peer],
            x_buf.at[group, half_count + place],
            a_send.at[group, step],
            a_recv.at[group, step],
            "tm",
            half * half_count + peer,
        )

    def frame_in(group, step):
        sender = lax.rem(place - step + half_count, half_count)
        return remote(
            a_buf.at[group, sender],
            x_buf.at[group, half_count + sender],
            a_send.at[group, step],
            a_recv.at[group, step],
            "tm",
            half * half_count + sender,
        )

    def later_out(group, step):
        peer = lax.rem(place + step, half_count)
        return remote(
            a_buf.at[group, peer],
            x_buf.at[group, place],
            l_send.at[group, step],
            l_recv.at[group, step],
            "tm",
            half_count + peer,
        )

    def earlier_in(group, step):
        sender = lax.rem(place - step + half_count, half_count)
        return remote(
            a_buf.at[group, sender],
            x_buf.at[group, sender],
            l_send.at[group, step],
            l_recv.at[group, step],
            "tm",
            sender,
        )

    def own_frame(group):
        return pltpu.make_async_copy(
            a_buf.at[group, place], x_buf.at[group, half_count + place], self_sem.at[group]
        )

    def take_group(group, sums):
        squares, b_in, c_out = sums

        def take_frame(step, carry):
            frame_in(group, step).wait_recv()
            return carry

        def take_earlier(step, carry):
            earlier_in(group, step).wait_recv()
            return carry

        lax.fori_loop(1, half_count, take_frame, 0)
        own_frame(group).wait()

        @pl.when(half == 1)
        def _():
            lax.fori_loop(0, half_count, take_earlier, 0)

        span = slice(group * width, (group + 1) * width)
        part = x_buf[group].astype(F32).reshape(2 * size, width)
        squares = squares + jnp.sum(part * part, axis=-1, keepdims=True)
        gained = (part * pre_ref[:, span]).astype(BF16)
        n_buf[group] = gained
        across = (((1,), (1,)), ((), ()))
        b_in = b_in + lax.dot_general(
            gained, w_in_ref[:, span], across, preferred_element_type=F32
        )
        c_out = c_out + lax.dot_general(
            gained[size:], w_out_ref[:, span], across, preferred_element_type=F32
        )
        return squares, b_in, c_out

    state = w_in_ref.shape[0]
    sums = (
        jnp.zeros((2 * size, 1), F32),
        jnp.zeros((2 * size, state), F32),
        jnp.zeros((size, state), F32),
    )
    for group in range(GROUPS):

        def relay(step, carry):
            direct_in(group, step).wait_recv()
            to_partner(group, step).start()
            return carry

        def relayed(step, carry):
            from_partner(group, step).wait_recv()
            return carry

        lax.fori_loop(1, chips, relay, 0)
        lax.fori_loop(0, chips, relayed, 0)
        for local in range(heads_here):
            lanes = slice(local * HEAD_DIM, (local + 1) * HEAD_DIM)
            head = group * heads_here + local
            query = q_ref[:, head * HEAD_DIM : (head + 1) * HEAD_DIM]
            key = kv_buf[group, :, 0, :, lanes].reshape(space_count * tokens, HEAD_DIM)
            value = kv_buf[group, :, 1, :, lanes].reshape(space_count * tokens, HEAD_DIM)
            scores = (
                lax.dot_general(
                    query, key, (((1,), (1,)), ((), ())), preferred_element_type=F32
                )
                * factor
                + bias
            )
            weights = jnp.exp2(scores - jnp.max(scores, axis=-1, keepdims=True))
            totals = jnp.sum(weights, axis=-1, keepdims=True)
            summed = jnp.dot(weights.astype(BF16), value, preferred_element_type=F32)
            attended = (summed / totals).reshape(half_count, rows, HEAD_DIM)
            a_buf[group, :, :, lanes] = attended.astype(BF16)

        def send_frame(step, carry):
            frame_out(group, step).start()
            return carry

        def send_later(step, carry):
            later_out(group, step).start()
            return carry

        @pl.when(half == 0)
        def _():
            lax.fori_loop(0, half_count, send_later, 0)

        lax.fori_loop(1, half_count, send_frame, 0)
        own_frame(group).start()
        if group >= LAG:
            sums = take_group(group - LAG, sums)

    for group in range(max(0, GROUPS - LAG), GROUPS):
        sums = take_group(group, sums)
    squares, b_in, c_out = sums
    scale = lax.rsqrt(squares / channels + 1e-05)
    across = (((1,), (1,)), ((), ()))
    gram = lax.dot_general(
        c_out * scale[size:], b_in * scale, across, precision=high, preferred_element_type=F32
    )
    gram = gram * jnp.transpose(jnp.broadcast_to(scale, (2 * size, size)))
    scale_own = scale[size:]
    squares = jnp.zeros((size, 1), F32)
    for head in range(SHARED_HEADS):
        group, local = head // heads_here, head % heads_here
        lanes = slice(local * HEAD_DIM, (local + 1) * HEAD_DIM)
        values = n_buf[group, :, lanes]
        mixing = (gram * d_buf[head]).astype(BF16)
        mixed = jnp.dot(mixing, values, preferred_element_type=F32)
        mixed = mixed + skips_ref[head] * scale_own * values[size:].astype(F32)
        y_buf[:, head * HEAD_DIM : (head + 1) * HEAD_DIM] = mixed
        squares = squares + jnp.sum(mixed * mixed, axis=-1, keepdims=True)
    scale = lax.rsqrt(squares / channels + 1e-05)
    result = y_buf[...] * scale * post_ref[...]
    o_buf[...] = result.reshape(half_count, rows, channels).astype(BF16)

    def result_out(step):
        peer = lax.rem(place + step, half_count)
        return remote(
            o_buf.at[peer],
            out_ref.at[place],
            o_send.at[step],
            o_recv.at[step],
            "tm",
            half * half_count + peer,
        )

    def result_in(step):
        sender = lax.rem(place - step + half_count, half_count)
        return remote(
            o_buf.at[sender],
            out_ref.at[sender],
            o_send.at[step],
            o_recv.at[step],
            "tm",
            half * half_count + sender,
        )

    def send_result(step, carry):
        result_out(step).start()
        return carry

    lax.fori_loop(1, half_count, send_result, 0)
    own_result = pltpu.make_async_copy(o_buf.at[place], out_ref.at[place], self_sem.at[GROUPS])
    own_result.start()

    for group in range(GROUPS):

        def sent_chip(step, carry):
            direct(group, step).wait_send()
            return carry

        def sent_partner(step, carry):
            to_partner(group, step).wait_send()
            return carry

        def sent_frame(step, carry):
            frame_out(group, step).wait_send()
            return carry

        lax.fori_loop(1, chips, sent_chip, 0)
        lax.fori_loop(0, chips, sent_partner, 0)
        lax.fori_loop(1, half_count, sent_frame, 0)

        def sent_later(step, carry):
            later_out(group, step).wait_send()
            return carry

        @pl.when(half == 0)
        def _():
            lax.fori_loop(0, half_count, sent_later, 0)

    for which in range(2):
        target = which * half_count + tm // 2

        @pl.when(target != tm)
        def _():
            step_copy(which, target, tm % 2).wait_send()


    def finish(step, carry):
        result_out(step).wait_send()
        result_in(step).wait_recv()
        return carry

    own_result.wait()
    lax.fori_loop(1, half_count, finish, 0)


def body(
    queries,
    key_vectors,
    value_vectors,
    block_lists,
    step_sizes,
    decay_rates,
    skip_gains,
    pre_gain,
    state_in_weight,
    state_out_weight,
    post_gain,
):
    tokens, channels = queries.shape[1], queries.shape[2]
    space_count = lax.axis_size("space")
    tm_count = lax.axis_size("tm")
    half_count = tm_count // 2
    rows = tokens // half_count
    width = channels // GROUPS
    chips = space_count // 2
    size = tokens
    state = state_in_weight.shape[1]
    hbm = pl.BlockSpec(memory_space=pl.ANY)
    dma = pltpu.SemaphoreType.DMA
    out = pl.pallas_call(
        functools.partial(kernel, (space_count, tm_count, block_lists.shape[1])),
        out_shape=jax.ShapeDtypeStruct((half_count, rows, channels), BF16),
        in_specs=[hbm] * 11,
        out_specs=hbm,
        scratch_shapes=[
            pltpu.SMEM(block_lists.shape, jnp.int32),
            pltpu.SMEM(decay_rates.shape, F32),
            pltpu.SMEM(skip_gains.shape, F32),
            pltpu.VMEM((tokens, channels), BF16),
            pltpu.VMEM((tm_count, 2, tokens // tm_count, SHARED_HEADS), F32),
            pltpu.VMEM((1, channels), F32),
            pltpu.VMEM((state, channels), BF16),
            pltpu.VMEM((state, channels), BF16),
            pltpu.VMEM((1, channels), F32),
            dma((8,)),
            dma((2,)),
            dma((2,)),
            dma((2,)),
            pltpu.VMEM((GROUPS, space_count, 2, tokens, width), BF16),
            pltpu.VMEM((GROUPS, half_count, rows, width), BF16),
            pltpu.VMEM((GROUPS, tm_count, rows, width), BF16),
            pltpu.VMEM((GROUPS, 2 * size, width), BF16),
            pltpu.VMEM((size, channels), F32),
            pltpu.VMEM((half_count, rows, channels), BF16),
            pltpu.VMEM((SHARED_HEADS, size, 2 * size), F32),
            dma((2, GROUPS)),
            dma((GROUPS, chips)),
            dma((GROUPS, chips)),
            dma((GROUPS, chips)),
            dma((GROUPS, chips)),
            dma((GROUPS, half_count)),
            dma((GROUPS, half_count)),
            dma((GROUPS, half_count)),
            dma((GROUPS, half_count)),
            dma((half_count,)),
            dma((half_count,)),
            dma((GROUPS + 1,)),
        ],
        compiler_params=pltpu.CompilerParams(
            collective_id=0, has_side_effects=True, vmem_limit_bytes=VMEM_BYTES
        ),
        name="attend_and_mix",
    )(
        block_lists,
        decay_rates,
        skip_gains,
        queries.reshape(tokens, channels),
        key_vectors.reshape(tokens, channels),
        value_vectors.reshape(tokens, channels),
        step_sizes,
        pre_gain.reshape(1, channels),
        state_in_weight.T,
        state_out_weight.T,
        post_gain.reshape(1, channels),
    )
    return out.reshape(1, tokens, channels)


def solution(mesh):
    placed = (
        P("tm", "space", None),
        P("tm", "space", None),
        P("tm", "space", None),
        P(),
        P(None, ("space", "tm"), None),
        P(),
        P(),
        P(),
        P(),
        P(),
        P(),
    )
    return jax.shard_map(
        body, mesh=mesh, in_specs=placed, out_specs=P("tm", "space", None), check_vma=False
    )
```
